32 devices in a mesh: layer: 4 (over x, core), lat: 8 (over z, y).
Axes of the slice: x: 2, y: 2, z: 4, core: 2. Of those that a mesh axis runs over, the one named last changes fastest.
Arguments:
- resid_in: bfloat16 [4, 4096, 256], P('layer', 'lat'), may hold values from -6 to 6
- resid_out: bfloat16 [4, 4096, 256], P('layer', 'lat'), may hold values from -80 to 80
- token_ids: int32 [256], replicated, may hold values from 0 to 128255, as said below
- active_mask: int32 [4, 6144, 256], P('layer', 'lat'), may hold values 0 or 1
- enc_weight: bfloat16 [4, 6144, 4096], P('layer', 'lat'), may hold values from -0.09375 to 0.09375
- enc_bias: bfloat16 [4, 6144], P('layer', 'lat'), may hold values from -3 to 3
- dec_weight: bfloat16 [4, 4, 6144, 4096], P('layer', None, 'lat'), may hold values from -0.078125 to 0.078125
- dec_bias: bfloat16 [4, 4096], P('layer', 'lat'), may hold values from -3 to 3
Outputs:
- enc_grad: bfloat16 [4, 6144, 4096], P('layer', 'lat')
- dec_grad: bfloat16 [4, 4, 6144, 4096], P('layer', None, 'lat')
- total_loss: float32 [], replicated
The draws below stay inside these ranges and needn't reach their ends.
Inputs may be any that keep to these rules, and one draw needn't show every extreme that they name: `token_ids`: ids of the Llama 3 vocabulary; the begin-of-text id 128000 stands at position 0 and at scattered other positions.
All inputs are finite; a program needn't handle non-finite values. No bound on the sum of `active_mask` on one device may be relied on, other than what follows from the above.
Results may differ from the reference program's by a relative error of at most 0.007.
Values may be sent and summed in bfloat16 or wider, within the bound.
A program may use at most 128 MiB of HBM per device.

```python
import math
import jax
import jax.numpy as jnp

D = 4096
M = 6144
TOK = 256
L = 4


def draw_token_ids(key, part):
    first_key, second_key = jax.random.split(jax.random.fold_in(key, 11))
    token_list = jax.random.randint(first_key, (TOK,), 0, 128256, dtype=jnp.int32)
    starting = jax.random.randint(second_key, (TOK,), 0, 8, dtype=jnp.int32) == 0
    token_list = jnp.where(starting, jnp.int32(128000), token_list)
    return token_list.at[0].set(jnp.int32(128000))


def draw_resid_out(key, part):
    base_key, feature_key, token_key = jax.random.split(jax.random.fold_in(key, 23), 3)
    base_values = jax.random.truncated_normal(base_key, -4.0, 4.0, (L, D, TOK), jnp.float32)
    feature_scale = jnp.exp(jax.random.uniform(feature_key, (L, D, 1), jnp.float32, 0.0, math.log(10.0)))
    token_scale = jnp.exp(jax.random.uniform(token_key, (1, 1, TOK), jnp.float32, 0.0, math.log(2.0)))
    return (base_values * feature_scale * token_scale).astype(jnp.bfloat16)


def plant(drawn, stream_key, low, largest):
    spot = [jax.random.randint(jax.random.fold_in(stream_key, axis), (), 0, length) for axis, length in enumerate(drawn.shape)]
    main_axis = drawn.shape.index(max(drawn.shape))
    next_to = spot[:main_axis] + [(spot[main_axis] + 1) % drawn.shape[main_axis]] + spot[main_axis + 1:]
    return drawn.at[tuple(spot)].set(low).at[tuple(next_to)].set(largest)


def levels(own_key, extent, shards, least, top_value):
    def one(position, blocks):
        steps = jax.random.uniform(jax.random.fold_in(jax.random.fold_in(own_key, 6), position), (blocks,), jnp.float32, least / len(shards), top_value / len(shards))
        return jnp.repeat(jnp.exp(steps), extent[position] // blocks).reshape((-1,) + (1,) * (len(extent) - position - 1))

    factor_of = one(*shards[0])
    for cut in shards[1:]:
        factor_of = factor_of * one(*cut)
    return factor_of


def normal_values(stream_key, dims, width, reach, cuts=(), kind=jnp.bfloat16):
    level = levels(stream_key, dims, cuts, -0.22, 0.18) if cuts else 1.0
    values = jax.random.normal(stream_key, dims, jnp.float32) * width * level
    return jnp.minimum(jnp.maximum(values, -reach), reach).astype(kind)


def setup_inputs(seed: int = 0) -> dict:
    splits = jax.random.split(jax.random.key(seed), 9)
    return {
        "resid_in": normal_values(splits[0], (L, D, TOK), 1.0, 6.0, ((0, 4), (1, 8))),
        "resid_out": draw_resid_out(jax.random.fold_in(splits[8], 71), 0),
        "token_ids": draw_token_ids(jax.random.fold_in(splits[8], 71), 0),
        "active_mask": plant((jax.random.randint(splits[3], (L, M, TOK), 0, 2) < 1).astype(jnp.int32), jax.random.fold_in(splits[3], 1), 0, 1),
        "enc_weight": normal_values(splits[4], (L, M, D), D ** -0.5, 0.09375, ((0, 4), (1, 8))),
        "enc_bias": normal_values(splits[5], (L, M), 0.5, 3.0, ((0, 4), (1, 8))),
        "dec_weight": normal_values(splits[6], (L, L, M, D), M ** -0.5, 0.078125, ((0, 4), (2, 8))),
        "dec_bias": normal_values(splits[7], (L, D), 0.5, 3.0, ((0, 4), (1, 8))),
    }


EPSILON = 1e-5


def reference(resid_in, resid_out, token_ids, active_mask, enc_weight, enc_bias, dec_weight, dec_bias):
    kept_tokens = (token_ids != 128000).astype(jnp.float32)
    latents = []
    gatings = []
    for layer in range(L):
        preact = jnp.dot(enc_weight[layer], resid_in[layer], preferred_element_type=jnp.float32)
        preact = preact + enc_bias[layer].astype(jnp.float32)[:, None]
        gating = active_mask[layer].astype(jnp.float32)
        gatings.append(gating)
        latents.append((gating * preact).astype(jnp.bfloat16))
    total_cells = D * TOK
    total_loss = jnp.zeros((), jnp.float32)
    out_grads = []
    for target in range(L):
        recon = jnp.zeros((D, TOK), jnp.float32) + dec_bias[target].astype(jnp.float32)[:, None]
        for source in range(target + 1):
            recon = recon + jnp.dot(dec_weight[target, source].T, latents[source], preferred_element_type=jnp.float32)
        wanted = resid_out[target].astype(jnp.float32)
        centered = wanted - jnp.mean(wanted, axis=1, keepdims=True)
        spread = jnp.sum(centered * centered) / total_cells + EPSILON
        residual_err = kept_tokens[None, :] * (recon - wanted)
        total_loss = total_loss + jnp.sum(residual_err * residual_err) / (2.0 * spread * total_cells)
        out_grads.append((residual_err / spread).astype(jnp.bfloat16))
    enc_rows = []
    for source in range(L):
        latent_grad = jnp.zeros((M, TOK), jnp.float32)
        for target in range(source, L):
            latent_grad = latent_grad + jnp.dot(dec_weight[target, source], out_grads[target], preferred_element_type=jnp.float32)
        preact_grad = (gatings[source] * latent_grad).astype(jnp.bfloat16)
        enc_rows.append(jnp.dot(preact_grad, resid_in[source].T, preferred_element_type=jnp.float32).astype(jnp.bfloat16))
    enc_grad = jnp.stack(enc_rows)
    dec_rows = []
    for target in range(L):
        row_list = []
        for source in range(L):
            if source <= target:
                row_list.append(jnp.dot(latents[source], out_grads[target].T, preferred_element_type=jnp.float32).astype(jnp.bfloat16))
            else:
                row_list.append(jnp.zeros((M, D), jnp.bfloat16))
        dec_rows.append(jnp.stack(row_list))
    dec_grad = jnp.stack(dec_rows)
    return enc_grad, dec_grad, total_loss
```

```python
import functools

import jax
import jax.numpy as jnp
from jax import lax
from jax.experimental import pallas as pl
from jax.experimental.pallas import tpu as pltpu
from jax.sharding import PartitionSpec as P

EPSILON = 1e-05
F32 = jnp.float32
BF16 = jnp.bfloat16


class Place:
    def __init__(self, lat_count):
        self.me = lax.axis_index("lat")
        self.depth = lat_count // 2
        self.z = self.me // 2
        self.y = self.me % 2
        self.partner = self.me + 1 - 2 * self.y
        self.has_up = self.z < self.depth - 1
        self.has_down = self.z > 0


def send(src, dst, send_sem, recv_sem, lat):
    return pltpu.make_async_remote_copy(
        src_ref=src,
        dst_ref=dst,
        send_sem=send_sem,
        recv_sem=recv_sem,
        device_id={"lat": lat},
        device_id_type=pl.DeviceIdType.MESH,
    )


def greet(at):
    barrier = pltpu.get_barrier_semaphore()

    def hello(lat):
        pl.semaphore_signal(
            barrier, inc=1, device_id={"lat": lat}, device_id_type=pl.DeviceIdType.MESH
        )

    hello(at.partner)
    pl.when(at.has_up)(lambda: hello(at.me + 2))
    pl.when(at.has_down)(lambda: hello(at.me - 2))
    peers = 1 + at.has_up.astype(jnp.int32) + at.has_down.astype(jnp.int32)
    pl.semaphore_wait(barrier, peers)


class Gather:
    def __init__(self, at, own, whole, sems):
        self.at, self.own, self.whole, self.sems = at, own, whole, sems

    def hop(self, kind, d):
        at = self.at
        shard = at.me - 2 * d if kind in (0, 2) else at.me + 2 * d
        src = self.own if d == 0 else self.whole.at[shard]
        to = (at.me + 2, at.me - 2, at.partner, at.partner)[kind]
        later = d + 1 if kind < 2 else d
        return send(
            src, self.whole.at[shard], self.sems.at[0, kind, d], self.sems.at[1, kind, later], to
        )

    def landing(self, kind, d):
        at = self.at
        below = kind in (0, 2)
        shard = at.me - 2 * d if below else at.me + 2 * d
        if kind >= 2:
            shard = shard + 1 - 2 * at.y
        ref = self.whole.at[shard]
        return send(ref, ref, self.sems.at[0, kind, d], self.sems.at[1, kind, d], at.partner)

    def start(self):
        pl.when(self.at.has_up)(lambda: self.hop(0, 0).start())
        pl.when(self.at.has_down)(lambda: self.hop(1, 0).start())
        self.hop(2, 0).start()

    def step(self, d):
        at = self.at

        @pl.when(at.z >= d)
        def _():
            self.landing(0, d).wait_recv()
            pl.when(at.has_up)(lambda: self.hop(0, d).start())
            self.hop(2, d).start()

        @pl.when(at.z + d < at.depth)
        def _():
            self.landing(1, d).wait_recv()
            pl.when(at.has_down)(lambda: self.hop(1, d).start())
            self.hop(3, d).start()

    def finish(self):
        at = self.at
        for d in range(at.depth):

            @pl.when(at.z >= d)
            def _():
                self.landing(2, d).wait_recv()
                self.hop(2, d).wait_send()
                if d < at.depth - 1:
                    pl.when(at.has_up)(lambda: self.hop(0, d).wait_send())

            @pl.when(at.z + d < at.depth)
            def _():
                if d > 0:
                    self.landing(3, d).wait_recv()
                    self.hop(3, d).wait_send()
                if d < at.depth - 1:
                    pl.when(at.has_down)(lambda: self.hop(1, d).wait_send())


def gather_kernel(lat_count, own, wanted_ref, whole, stats, stat, big_sems, stat_sems, local_sem):
    at = Place(lat_count)
    greet(at)
    big = Gather(at, own, whole, big_sems)
    big.start()
    keep = pltpu.make_async_copy(own, whole.at[at.me], local_sem)
    keep.start()
    wanted = wanted_ref[...].astype(F32)
    centered = wanted - jnp.mean(wanted, axis=1, keepdims=True)
    total = jnp.sum(centered * centered, keepdims=True)
    stat[...] = jnp.broadcast_to(total, stat.shape)
    stats[at.me] = stat[...]
    small = Gather(at, stat, stats, stat_sems)
    small.start()
    for d in range(1, at.depth):
        big.step(d)
        small.step(d)
    keep.wait()
    big.finish()
    small.finish()


def reduce_kernel(
    lat_count,
    parts,
    wanted_ref,
    bias_ref,
    kept_ref,
    spread_ref,
    whole,
    stats,
    across_up,
    across_down,
    from_below,
    from_above,
    going_up,
    going_down,
    total,
    grad,
    stat,
    across_sems,
    line_sems,
    big_sems,
    stat_sems,
):
    at = Place(lat_count)
    depth = at.depth
    greet(at)

    def across(up, d):
        rung = at.z + d if up else at.z - d
        row = 0 if up else 1
        return send(
            parts.at[rung * 2 + 1 - at.y],
            (across_up if up else across_down).at[d],
            across_sems.at[0, row, d],
            across_sems.at[1, row, d],
            at.partner,
        )

    def along(up, d):
        row = 0 if up else 1
        return send(
            (going_up if up else going_down).at[d],
            (from_below if up else from_above).at[d - 1],
            line_sems.at[0, row, d],
            line_sems.at[1, row, d - 1],
            at.me + 2 if up else at.me - 2,
        )

    def arrived(up, d):
        row = 0 if up else 1
        ref = (from_below if up else from_above).at[d]
        send(ref, ref, line_sems.at[0, row, d], line_sems.at[1, row, d], at.partner).wait_recv()

    for d in range(depth - 1, -1, -1):
        pl.when(at.z + d < depth)(lambda: across(True, d).start())
        if d:
            pl.when(at.z >= d)(lambda: across(False, d).start())

    def forward(up, d):
        across(up, d).wait_recv()
        rung = at.z + d if up else at.z - d
        crossed = across_up if up else across_down
        came = from_below if up else from_above
        going = going_up if up else going_down
        behind = at.has_down if up else at.has_up
        mine = parts.at[rung * 2 + at.y]

        @pl.when(behind)
        def _():
            if d < depth - 1:
                arrived(up, d)
                going[d] = (
                    mine[...].astype(F32) + crossed[d].astype(F32) + came[d].astype(F32)
                ).astype(BF16)

        @pl.when(jnp.logical_not(behind))
        def _():
            going[d] = (mine[...].astype(F32) + crossed[d].astype(F32)).astype(BF16)

        along(up, d).start()

    for d in range(depth - 1, 0, -1):
        pl.when(at.z + d < depth)(lambda: forward(True, d))
        pl.when(at.z >= d)(lambda: forward(False, d))
    across(True, 0).wait_recv()
    total[...] = (
        parts[at.me].astype(F32)
        + across_up[0].astype(F32)
        + (bias_ref[...] - wanted_ref[...].astype(F32))
    )

    @pl.when(at.has_down)
    def _():
        arrived(True, 0)
        total[...] += from_below[0].astype(F32)

    @pl.when(at.has_up)
    def _():
        arrived(False, 0)
        total[...] += from_above[0].astype(F32)

    err = kept_ref[...] * total[...]
    grad[...] = (err / spread_ref[...]).astype(BF16)
    whole[at.me] = grad[...]
    big = Gather(at, grad, whole, big_sems)
    big.start()
    stat[...] = jnp.broadcast_to(jnp.sum(err * err, keepdims=True), stat.shape)
    stats[at.me] = stat[...]
    small = Gather(at, stat, stats, stat_sems)
    small.start()
    for d in range(1, depth):
        big.step(d)
        small.step(d)
    big.finish()
    small.finish()
    for d in range(depth - 1, -1, -1):

        @pl.when(at.z + d < depth)
        def _():
            across(True, d).wait_send()
            if d:
                along(True, d).wait_send()

        if d:

            @pl.when(at.z >= d)
            def _():
                across(False, d).wait_send()
                along(False, d).wait_send()


VMEM = pl.BlockSpec(memory_space=pltpu.VMEM)


def gather_inputs(inputs_local, wanted, lat_count):
    rows, tokens = inputs_local.shape
    depth = lat_count // 2
    return pl.pallas_call(
        functools.partial(gather_kernel, lat_count),
        out_shape=(
            jax.ShapeDtypeStruct((lat_count, rows, tokens), BF16),
            jax.ShapeDtypeStruct((lat_count, 8, 128), F32),
        ),
        in_specs=[VMEM] * 2,
        out_specs=(VMEM, VMEM),
        scratch_shapes=[
            pltpu.VMEM((8, 128), F32),
            pltpu.SemaphoreType.DMA((2, 4, depth + 1)),
            pltpu.SemaphoreType.DMA((2, 4, depth + 1)),
            pltpu.SemaphoreType.DMA,
        ],
        compiler_params=pltpu.CompilerParams(
            collective_id=0, has_side_effects=True, vmem_limit_bytes=32 << 20
        ),
    )(inputs_local, wanted)


def reduce_and_gather(parts, wanted, bias, kept, spread, lat_count):
    _, rows, tokens = parts.shape
    depth = lat_count // 2
    slots = pltpu.VMEM((depth, rows, tokens), BF16)
    return pl.pallas_call(
        functools.partial(reduce_kernel, lat_count),
        out_shape=(
            jax.ShapeDtypeStruct((lat_count, rows, tokens), BF16),
            jax.ShapeDtypeStruct((lat_count, 8, 128), F32),
        ),
        in_specs=[VMEM] * 5,
        out_specs=(VMEM, VMEM),
        scratch_shapes=[slots] * 6
        + [
            pltpu.VMEM((rows, tokens), F32),
            pltpu.VMEM((rows, tokens), BF16),
            pltpu.VMEM((8, 128), F32),
            pltpu.SemaphoreType.DMA((2, 2, depth)),
            pltpu.SemaphoreType.DMA((2, 2, depth)),
            pltpu.SemaphoreType.DMA((2, 4, depth + 1)),
            pltpu.SemaphoreType.DMA((2, 4, depth + 1)),
        ],
        compiler_params=pltpu.CompilerParams(
            collective_id=1, has_side_effects=True, vmem_limit_bytes=40 << 20
        ),
    )(parts, wanted, bias, kept, spread)


def on_device(
    resid_in, resid_out, token_ids, active_mask, enc_weight, enc_bias, dec_weight, dec_bias
):
    layer_count = lax.axis_size("layer")
    lat_count = lax.axis_size("lat")
    layer_here = lax.axis_index("layer")
    inputs_local = resid_in[0]
    wanted = resid_out[0]
    weight_enc = enc_weight[0]
    lat_rows = weight_enc.shape[0]
    feature_count = weight_enc.shape[1]
    feature_rows, token_count = inputs_local.shape
    total_cells = feature_count * token_count
    whole_inputs, target_stats = gather_inputs(inputs_local, wanted, lat_count)
    whole_inputs = whole_inputs.reshape(feature_count, token_count)
    spread = jnp.sum(target_stats[:, 0, 0]) / total_cells + EPSILON
    preact = jnp.dot(weight_enc, whole_inputs, preferred_element_type=F32)
    preact = preact + enc_bias[0].astype(F32)[:, None]
    gating = active_mask[0].astype(F32)
    latents = (gating * preact).astype(BF16)
    source_ids = jnp.arange(layer_count)
    gathered = lax.all_gather(latents[None], "layer", axis=0, tiled=True)
    acts_stack = jnp.where(
        (source_ids <= layer_here)[:, None, None], gathered, jnp.zeros((), BF16)
    )
    stack_rows = acts_stack.reshape(layer_count * lat_rows, token_count)
    weight_rows = dec_weight[0].reshape(layer_count * lat_rows, feature_count)
    kept_tokens = (token_ids != 128000).astype(F32)
    parts = lax.dot_general(
        weight_rows, stack_rows, (((0,), (0,)), ((), ())), preferred_element_type=F32
    ).astype(BF16)
    full_grad, err_stats = reduce_and_gather(
        parts.reshape(lat_count, feature_rows, token_count),
        wanted,
        dec_bias[0].astype(F32)[:, None],
        kept_tokens[None, :],
        jnp.broadcast_to(spread, (1, token_count)),
        lat_count,
    )
    full_grad = full_grad.reshape(feature_count, token_count)
    layer_loss = jnp.sum(err_stats[:, 0, 0]) / (2.0 * spread * total_cells)
    total_loss = lax.psum(layer_loss, "layer")
    grad_rows = jnp.dot(weight_rows, full_grad, preferred_element_type=F32).reshape(
        layer_count, lat_rows, token_count
    )
    grad_rows = (grad_rows * (source_ids <= layer_here).astype(F32)[:, None, None]).astype(BF16)
    dec_out = lax.dot_general(
        stack_rows, full_grad, (((1,), (1,)), ((), ())), preferred_element_type=F32
    )
    dec_out = dec_out.astype(BF16).reshape(1, layer_count, lat_rows, feature_count)
    latent_grad = lax.psum_scatter(grad_rows, "layer", scatter_dimension=0, tiled=True)[0]
    preact_grad = (gating * latent_grad.astype(F32)).astype(BF16)
    enc_out = lax.dot_general(
        preact_grad, whole_inputs, (((1,), (1,)), ((), ())), preferred_element_type=F32
    )
    return (enc_out.astype(BF16)[None], dec_out, total_loss)


def solution(mesh):
    in_specs = (
        P("layer", "lat", None),
        P("layer", "lat", None),
        P(),
        P("layer", "lat", None),
        P("layer", "lat", None),
        P("layer", "lat"),
        P("layer", None, "lat", None),
        P("layer", "lat"),
    )
    out_specs = (P("layer", "lat", None), P("layer", None, "lat", None), P())
    return jax.shard_map(
        on_device, mesh=mesh, in_specs=in_specs, out_specs=out_specs, check_vma=False
    )
```

```python
import functools

import jax
import jax.numpy as jnp
from jax import lax
from jax.experimental import pallas as pl
from jax.experimental.pallas import tpu as pltpu
from jax.sharding import PartitionSpec as P

EPSILON = 1e-05
F32 = jnp.float32
BF16 = jnp.bfloat16


class Place:
    def __init__(self, lat_count):
        self.me = lax.axis_index("lat")
        self.depth = lat_count // 2
        self.z = self.me // 2
        self.y = self.me % 2
        self.partner = self.me + 1 - 2 * self.y
        self.has_up = self.z < self.depth - 1
        self.has_down = self.z > 0


def send(src, dst, send_sem, recv_sem, lat):
    return pltpu.make_async_remote_copy(
        src_ref=src,
        dst_ref=dst,
        send_sem=send_sem,
        recv_sem=recv_sem,
        device_id={"lat": lat},
        device_id_type=pl.DeviceIdType.MESH,
    )


def greet(at, more=0):
    barrier = pltpu.get_barrier_semaphore()

    def hello(lat):
        pl.semaphore_signal(
            barrier, inc=1, device_id={"lat": lat}, device_id_type=pl.DeviceIdType.MESH
        )

    hello(at.partner)
    pl.when(at.has_up)(lambda: hello(at.me + 2))
    pl.when(at.has_down)(lambda: hello(at.me - 2))
    peers = 1 + more + at.has_up.astype(jnp.int32) + at.has_down.astype(jnp.int32)
    pl.semaphore_wait(barrier, peers)


class Gather:
    def __init__(self, at, own, whole, sems):
        self.at, self.own, self.whole, self.sems = at, own, whole, sems

    def hop(self, kind, d):
        at = self.at
        shard = at.me - 2 * d if kind in (0, 2) else at.me + 2 * d
        src = self.own if d == 0 else self.whole.at[shard]
        to = (at.me + 2, at.me - 2, at.partner, at.partner)[kind]
        later = d + 1 if kind < 2 else d
        return send(
            src, self.whole.at[shard], self.sems.at[0, kind, d], self.sems.at[1, kind, later], to
        )

    def landing(self, kind, d):
        at = self.at
        below = kind in (0, 2)
        shard = at.me - 2 * d if below else at.me + 2 * d
        if kind >= 2:
            shard = shard + 1 - 2 * at.y
        ref = self.whole.at[shard]
        return send(ref, ref, self.sems.at[0, kind, d], self.sems.at[1, kind, d], at.partner)

    def start(self):
        pl.when(self.at.has_up)(lambda: self.hop(0, 0).start())
        pl.when(self.at.has_down)(lambda: self.hop(1, 0).start())
        self.hop(2, 0).start()

    def step(self, d):
        at = self.at

        @pl.when(at.z >= d)
        def _():
            self.landing(0, d).wait_recv()
            pl.when(at.has_up)(lambda: self.hop(0, d).start())
            self.hop(2, d).start()

        @pl.when(at.z + d < at.depth)
        def _():
            self.landing(1, d).wait_recv()
            pl.when(at.has_down)(lambda: self.hop(1, d).start())
            self.hop(3, d).start()

    def finish(self, crossed=False):
        at = self.at
        for d in range(at.depth):

            @pl.when(at.z >= d)
            def _():
                if not crossed:
                    self.landing(2, d).wait_recv()
                self.hop(2, d).wait_send()
                if d < at.depth - 1:
                    pl.when(at.has_up)(lambda: self.hop(0, d).wait_send())

            @pl.when(at.z + d < at.depth)
            def _():
                if d > 0:
                    if not crossed:
                        self.landing(3, d).wait_recv()
                    self.hop(3, d).wait_send()
                if d < at.depth - 1:
                    pl.when(at.has_down)(lambda: self.hop(1, d).wait_send())


def gather_kernel(lat_count, own, wanted_ref, whole, stats, stat, big_sems, stat_sems, local_sem):
    at = Place(lat_count)
    greet(at)
    big = Gather(at, own, whole, big_sems)
    big.start()
    keep = pltpu.make_async_copy(own, whole.at[at.me], local_sem)
    keep.start()
    wanted = wanted_ref[...].astype(F32)
    centered = wanted - jnp.mean(wanted, axis=1, keepdims=True)
    total = jnp.sum(centered * centered, keepdims=True)
    stat[...] = jnp.broadcast_to(total, stat.shape)
    stats[at.me] = stat[...]
    small = Gather(at, stat, stats, stat_sems)
    small.start()
    for d in range(1, at.depth):
        big.step(d)
        small.step(d)
    keep.wait()
    big.finish()
    small.finish()


def reduce_kernel(
    lat_count,
    parts,
    wanted_ref,
    bias_ref,
    kept_ref,
    spread_ref,
    whole,
    stats,
    across_up,
    across_down,
    from_below,
    from_above,
    going_up,
    going_down,
    total,
    grad,
    stat,
    across_sems,
    line_sems,
    big_sems,
    stat_sems,
):
    at = Place(lat_count)
    depth = at.depth
    greet(at)

    def across(up, d):
        rung = at.z + d if up else at.z - d
        row = 0 if up else 1
        return send(
            parts.at[rung * 2 + 1 - at.y],
            (across_up if up else across_down).at[d],
            across_sems.at[0, row, d],
            across_sems.at[1, row, d],
            at.partner,
        )

    def along(up, d):
        row = 0 if up else 1
        return send(
            (going_up if up else going_down).at[d],
            (from_below if up else from_above).at[d - 1],
            line_sems.at[0, row, d],
            line_sems.at[1, row, d - 1],
            at.me + 2 if up else at.me - 2,
        )

    def arrived(up, d):
        row = 0 if up else 1
        ref = (from_below if up else from_above).at[d]
        send(ref, ref, line_sems.at[0, row, d], line_sems.at[1, row, d], at.partner).wait_recv()

    for d in range(depth - 1, -1, -1):
        pl.when(at.z + d < depth)(lambda: across(True, d).start())
        if d:
            pl.when(at.z >= d)(lambda: across(False, d).start())

    def forward(up, d):
        across(up, d).wait_recv()
        rung = at.z + d if up else at.z - d
        crossed = across_up if up else across_down
        came = from_below if up else from_above
        going = going_up if up else going_down
        behind = at.has_down if up else at.has_up
        mine = parts.at[rung * 2 + at.y]

        @pl.when(behind)
        def _():
            if d < depth - 1:
                arrived(up, d)
                going[d] = (
                    mine[...].astype(F32) + crossed[d].astype(F32) + came[d].astype(F32)
                ).astype(BF16)

        @pl.when(jnp.logical_not(behind))
        def _():
            going[d] = (mine[...].astype(F32) + crossed[d].astype(F32)).astype(BF16)

        along(up, d).start()

    for d in range(depth - 1, 0, -1):
        pl.when(at.z + d < depth)(lambda: forward(True, d))
        pl.when(at.z >= d)(lambda: forward(False, d))
    across(True, 0).wait_recv()
    total[...] = (
        parts[at.me].astype(F32)
        + across_up[0].astype(F32)
        + (bias_ref[...] - wanted_ref[...].astype(F32))
    )

    @pl.when(at.has_down)
    def _():
        arrived(True, 0)
        total[...] += from_below[0].astype(F32)

    @pl.when(at.has_up)
    def _():
        arrived(False, 0)
        total[...] += from_above[0].astype(F32)

    err = kept_ref[...] * total[...]
    grad[...] = (err / spread_ref[...]).astype(BF16)
    whole[at.me] = grad[...]
    big = Gather(at, grad, whole, big_sems)
    big.start()
    stat[...] = jnp.broadcast_to(jnp.sum(err * err, keepdims=True), stat.shape)
    stats[at.me] = stat[...]
    small = Gather(at, stat, stats, stat_sems)
    small.start()
    for d in range(1, depth):
        big.step(d)
        small.step(d)
    big.finish()
    small.finish()
    for d in range(depth - 1, -1, -1):

        @pl.when(at.z + d < depth)
        def _():
            across(True, d).wait_send()
            if d:
                along(True, d).wait_send()

        if d:

            @pl.when(at.z >= d)
            def _():
                across(False, d).wait_send()
                along(False, d).wait_send()


def flow(at, gathers, use):
    use(at.me)

    def cross(d):
        @pl.when(at.z >= d)
        def _():
            for one in gathers:
                one.landing(2, d).wait_recv()
            use(at.partner - 2 * d)

        if d:

            @pl.when(at.z + d < at.depth)
            def _():
                for one in gathers:
                    one.landing(3, d).wait_recv()
                use(at.partner + 2 * d)

    for d in range(1, at.depth):
        for one in gathers:
            one.step(d)
        pl.when(at.z >= d)(lambda: use(at.me - 2 * d))
        pl.when(at.z + d < at.depth)(lambda: use(at.me + 2 * d))
        cross(d - 1)
    cross(at.depth - 1)
    for one in gathers:
        one.finish(crossed=True)


def to_layer(src, dst, send_sem, recv_sem, layer):
    return pltpu.make_async_remote_copy(
        src_ref=src,
        dst_ref=dst,
        send_sem=send_sem,
        recv_sem=recv_sem,
        device_id={"layer": layer},
        device_id_type=pl.DeviceIdType.MESH,
    )


def encode_kernel(
    lat_count,
    layer_count,
    own,
    wanted_ref,
    weight,
    bias_ref,
    gate_ref,
    whole,
    stats,
    acts,
    stat,
    blocks,
    acc,
    big_sems,
    stat_sems,
    local_sem,
    block_sems,
    layer_sems,
):
    at = Place(lat_count)
    rows = own.shape[0]
    pairs = layer_count // 2
    layer = lax.axis_index("layer")
    pair, core = layer // 2, layer % 2
    mate = layer + 1 - 2 * core

    def load(g):
        return pltpu.make_async_copy(
            weight.at[:, pl.ds(g * rows, rows)], blocks.at[g], block_sems.at[g]
        )

    for g in range(lat_count):
        load(g).start()
    barrier = pltpu.get_barrier_semaphore()
    for k in range(1, pairs):
        other = lax.rem(pair + k, pairs) * 2 + core
        pl.semaphore_signal(
            barrier, inc=1, device_id={"layer": other}, device_id_type=pl.DeviceIdType.MESH
        )
    pl.semaphore_signal(
        barrier, inc=1, device_id={"layer": mate}, device_id_type=pl.DeviceIdType.MESH
    )
    greet(at, pairs)
    big = Gather(at, own, whole, big_sems)
    big.start()
    keep = pltpu.make_async_copy(own, whole.at[at.me], local_sem)
    keep.start()
    wanted = wanted_ref[...].astype(F32)
    centered = wanted - jnp.mean(wanted, axis=1, keepdims=True)
    spread = jnp.sum(centered * centered, keepdims=True)
    stat[...] = jnp.broadcast_to(spread, stat.shape)
    stats[at.me] = stat[...]
    small = Gather(at, stat, stats, stat_sems)
    small.start()
    acc[...] = jnp.broadcast_to(bias_ref[...], acc.shape)
    for g in range(lat_count):
        load(g).wait()
    keep.wait()

    def use(g):
        acc[...] += jnp.dot(blocks[g], whole[g], preferred_element_type=F32)

    flow(at, (big, small), use)
    acts[layer] = (gate_ref[...].astype(F32) * acc[...]).astype(BF16)

    def over(k):
        ref = acts.at[layer]
        return to_layer(
            ref, ref, layer_sems.at[0, 0, k], layer_sems.at[1, 0, k], layer + 2 * k
        )

    def pass_on(k):
        ref = acts.at[layer - 2 * k]
        return to_layer(ref, ref, layer_sems.at[0, 1, k], layer_sems.at[1, 1, k], mate)

    def landed(kind, k):
        ref = acts.at[layer - 2 * k if kind == 0 else mate - 2 * k]
        sem = layer_sems.at[1, kind, k]
        return to_layer(ref, ref, layer_sems.at[0, kind, k], sem, mate)

    for k in range(1, pairs):
        pl.when(pair + k < pairs)(lambda: over(k).start())
    pl.when(core == 0)(lambda: pass_on(0).start())
    for k in range(1, pairs):

        @pl.when(pair + k < pairs)
        def _():
            empty = jnp.zeros(acts.shape[1:], BF16)
            acts[layer + 2 * k] = empty
            acts[mate + 2 * k] = empty

    @pl.when(core == 0)
    def _():
        acts[mate] = jnp.zeros(acts.shape[1:], BF16)

    for k in range(1, pairs):

        @pl.when(pair >= k)
        def _():
            landed(0, k).wait_recv()
            pass_on(k).start()

    pl.when(core == 1)(lambda: landed(1, 0).wait_recv())
    for k in range(1, pairs):

        @pl.when(pair >= k)
        def _():
            landed(1, k).wait_recv()
            pass_on(k).wait_send()

        pl.when(pair + k < pairs)(lambda: over(k).wait_send())
    pl.when(core == 0)(lambda: pass_on(0).wait_send())


def decode_kernel(
    lat_count,
    weight,
    acts,
    wanted_ref,
    bias_ref,
    kept_ref,
    spread_ref,
    whole,
    stats,
    rows_out,
    blocks,
    turned,
    leaving_up,
    leaving_down,
    across_up,
    across_down,
    from_below,
    from_above,
    going_up,
    going_down,
    total,
    grad,
    stat,
    acc,
    block_sems,
    across_sems,
    line_sems,
    big_sems,
    stat_sems,
):
    at = Place(lat_count)
    depth = at.depth
    layer_count, lat_rows, tokens = acts.shape
    width = blocks.shape[3]
    layer = lax.axis_index("layer")

    def load(g):
        columns = pl.ds(pl.multiple_of(g * width, width), width)
        return pltpu.make_async_copy(weight.at[:, :, columns], blocks.at[g], block_sems.at[g])

    for cross in (True, False):
        for d in range(depth - 1, -1, -1):
            mine = at.partner if cross else at.me
            pl.when(at.z + d < depth)(lambda: load(mine + 2 * d).start())
            if d:
                pl.when(at.z >= d)(lambda: load(mine - 2 * d).start())
    greet(at)
    for source in range(layer_count):
        turned[source] = jnp.transpose(acts[source])

    def part(g):
        load(g).wait()
        got = jnp.dot(turned[0], blocks[g, 0], preferred_element_type=F32)
        for source in range(1, layer_count):
            got += jnp.dot(turned[source], blocks[g, source], preferred_element_type=F32)
        return got

    def across(up, d):
        row = 0 if up else 1
        return send(
            (leaving_up if up else leaving_down).at[d],
            (across_up if up else across_down).at[d],
            across_sems.at[0, row, d],
            across_sems.at[1, row, d],
            at.partner,
        )

    def along(up, d):
        row = 0 if up else 1
        return send(
            (going_up if up else going_down).at[d],
            (from_below if up else from_above).at[d - 1],
            line_sems.at[0, row, d],
            line_sems.at[1, row, d - 1],
            at.me + 2 if up else at.me - 2,
        )

    def arrived(up, d):
        row = 0 if up else 1
        ref = (from_below if up else from_above).at[d]
        send(ref, ref, line_sems.at[0, row, d], line_sems.at[1, row, d], at.partner).wait_recv()

    def leave(up, d):
        made = part(at.partner + 2 * d if up else at.partner - 2 * d)
        (leaving_up if up else leaving_down)[d] = made.astype(BF16)
        across(up, d).start()

    for d in range(depth - 1, -1, -1):
        pl.when(at.z + d < depth)(lambda: leave(True, d))
        if d:
            pl.when(at.z >= d)(lambda: leave(False, d))

    def forward(up, d):
        total[...] = part(at.me + 2 * d if up else at.me - 2 * d)
        across(up, d).wait_recv()
        total[...] += (across_up if up else across_down)[d].astype(F32)
        if d < depth - 1:

            @pl.when(at.has_down if up else at.has_up)
            def _():
                arrived(up, d)
                total[...] += (from_below if up else from_above)[d].astype(F32)

        (going_up if up else going_down)[d] = total[...].astype(BF16)
        along(up, d).start()

    for d in range(depth - 1, 0, -1):
        pl.when(at.z + d < depth)(lambda: forward(True, d))
        pl.when(at.z >= d)(lambda: forward(False, d))
    total[...] = part(at.me) + bias_ref[...] - jnp.transpose(wanted_ref[...].astype(F32))
    across(True, 0).wait_recv()
    total[...] += across_up[0].astype(F32)

    @pl.when(at.has_down)
    def _():
        arrived(True, 0)
        total[...] += from_below[0].astype(F32)

    @pl.when(at.has_up)
    def _():
        arrived(False, 0)
        total[...] += from_above[0].astype(F32)

    err = kept_ref[...] * total[...]
    grad[...] = jnp.transpose(err / spread_ref[...]).astype(BF16)
    big = Gather(at, grad, whole, big_sems)
    big.start()
    whole[at.me] = grad[...]
    stat[...] = jnp.broadcast_to(jnp.sum(err * err, keepdims=True), stat.shape)
    stats[at.me] = stat[...]
    small = Gather(at, stat, stats, stat_sems)
    small.start()
    acc[...] = jnp.zeros_like(acc)

    def use(g):
        @pl.loop(0, layer_count)
        def _(source):
            acc[source] += jnp.dot(blocks[g, source], whole[g], preferred_element_type=F32)

    flow(at, (big, small), use)
    for source in range(layer_count):
        wanted_here = (source <= layer).astype(F32)
        rows_out[source] = (acc[source] * wanted_here).astype(BF16)
    for d in range(depth - 1, -1, -1):

        @pl.when(at.z + d < depth)
        def _():
            across(True, d).wait_send()
            if d:
                along(True, d).wait_send()

        if d:

            @pl.when(at.z >= d)
            def _():
                across(False, d).wait_send()
                along(False, d).wait_send()


VMEM = pl.BlockSpec(memory_space=pltpu.VMEM)
HBM = pl.BlockSpec(memory_space=pl.ANY)


def encode(inputs_local, wanted, weight, bias, gate, lat_count, layer_count):
    rows, tokens = inputs_local.shape
    lat_rows = weight.shape[0]
    depth = lat_count // 2
    return pl.pallas_call(
        functools.partial(encode_kernel, lat_count, layer_count),
        out_shape=(
            jax.ShapeDtypeStruct((lat_count, rows, tokens), BF16),
            jax.ShapeDtypeStruct((lat_count, 8, 128), F32),
            jax.ShapeDtypeStruct((layer_count, lat_rows, tokens), BF16),
        ),
        in_specs=[VMEM, VMEM, HBM, VMEM, VMEM],
        out_specs=(VMEM,) * 3,
        scratch_shapes=[
            pltpu.VMEM((8, 128), F32),
            pltpu.VMEM((lat_count, lat_rows, rows), BF16),
            pltpu.VMEM((lat_rows, tokens), F32),
            pltpu.SemaphoreType.DMA((2, 4, depth + 1)),
            pltpu.SemaphoreType.DMA((2, 4, depth + 1)),
            pltpu.SemaphoreType.DMA,
            pltpu.SemaphoreType.DMA((lat_count,)),
            pltpu.SemaphoreType.DMA((2, 2, layer_count // 2)),
        ],
        compiler_params=pltpu.CompilerParams(
            collective_id=2, has_side_effects=True, vmem_limit_bytes=40 << 20
        ),
    )(inputs_local, wanted, weight, bias, gate)


def decode(weight, acts, wanted, bias, kept, spread, lat_count):
    layer_count, lat_rows, tokens = acts.shape
    rows = wanted.shape[0]
    depth = lat_count // 2
    slots = pltpu.VMEM((depth, tokens, rows), BF16)
    return pl.pallas_call(
        functools.partial(decode_kernel, lat_count),
        out_shape=(
            jax.ShapeDtypeStruct((lat_count, rows, tokens), BF16),
            jax.ShapeDtypeStruct((lat_count, 8, 128), F32),
            jax.ShapeDtypeStruct((layer_count, lat_rows, tokens), BF16),
        ),
        in_specs=[HBM] + [VMEM] * 5,
        out_specs=(VMEM,) * 3,
        scratch_shapes=[
            pltpu.VMEM((lat_count, layer_count, lat_rows, rows), BF16),
            pltpu.VMEM((layer_count, tokens, lat_rows), BF16),
        ]
        + [slots] * 8
        + [
            pltpu.VMEM((tokens, rows), F32),
            pltpu.VMEM((rows, tokens), BF16),
            pltpu.VMEM((8, 128), F32),
            pltpu.VMEM((layer_count, lat_rows, tokens), F32),
            pltpu.SemaphoreType.DMA((lat_count,)),
            pltpu.SemaphoreType.DMA((2, 2, depth)),
            pltpu.SemaphoreType.DMA((2, 2, depth)),
            pltpu.SemaphoreType.DMA((2, 4, depth + 1)),
            pltpu.SemaphoreType.DMA((2, 4, depth + 1)),
        ],
        compiler_params=pltpu.CompilerParams(
            collective_id=3, has_side_effects=True, vmem_limit_bytes=58 << 20
        ),
    )(weight, acts, wanted, bias, kept, spread)


def gather_inputs(inputs_local, wanted, lat_count):
    rows, tokens = inputs_local.shape
    depth = lat_count // 2
    return pl.pallas_call(
        functools.partial(gather_kernel, lat_count),
        out_shape=(
            jax.ShapeDtypeStruct((lat_count, rows, tokens), BF16),
            jax.ShapeDtypeStruct((lat_count, 8, 128), F32),
        ),
        in_specs=[VMEM] * 2,
        out_specs=(VMEM, VMEM),
        scratch_shapes=[
            pltpu.VMEM((8, 128), F32),
            pltpu.SemaphoreType.DMA((2, 4, depth + 1)),
            pltpu.SemaphoreType.DMA((2, 4, depth + 1)),
            pltpu.SemaphoreType.DMA,
        ],
        compiler_params=pltpu.CompilerParams(
            collective_id=0, has_side_effects=True, vmem_limit_bytes=32 << 20
        ),
    )(inputs_local, wanted)


def reduce_and_gather(parts, wanted, bias, kept, spread, lat_count):
    _, rows, tokens = parts.shape
    depth = lat_count // 2
    slots = pltpu.VMEM((depth, rows, tokens), BF16)
    return pl.pallas_call(
        functools.partial(reduce_kernel, lat_count),
        out_shape=(
            jax.ShapeDtypeStruct((lat_count, rows, tokens), BF16),
            jax.ShapeDtypeStruct((lat_count, 8, 128), F32),
        ),
        in_specs=[VMEM] * 5,
        out_specs=(VMEM, VMEM),
        scratch_shapes=[slots] * 6
        + [
            pltpu.VMEM((rows, tokens), F32),
            pltpu.VMEM((rows, tokens), BF16),
            pltpu.VMEM((8, 128), F32),
            pltpu.SemaphoreType.DMA((2, 2, depth)),
            pltpu.SemaphoreType.DMA((2, 2, depth)),
            pltpu.SemaphoreType.DMA((2, 4, depth + 1)),
            pltpu.SemaphoreType.DMA((2, 4, depth + 1)),
        ],
        compiler_params=pltpu.CompilerParams(
            collective_id=1, has_side_effects=True, vmem_limit_bytes=40 << 20
        ),
    )(parts, wanted, bias, kept, spread)


def on_device(
    resid_in, resid_out, token_ids, active_mask, enc_weight, enc_bias, dec_weight, dec_bias
):
    layer_count = lax.axis_size("layer")
    lat_count = lax.axis_size("lat")
    layer_here = lax.axis_index("layer")
    inputs_local = resid_in[0]
    wanted = resid_out[0]
    weight_enc = enc_weight[0]
    lat_rows = weight_enc.shape[0]
    feature_count = weight_enc.shape[1]
    feature_rows, token_count = inputs_local.shape
    total_cells = feature_count * token_count
    kept_tokens = (token_ids != 128000).astype(F32)
    source_ids = jnp.arange(layer_count)
    gating = active_mask[0].astype(F32)
    weight_rows = dec_weight[0].reshape(layer_count * lat_rows, feature_count)
    fused = feature_rows % 128 == 0 and lat_rows % 128 == 0 and layer_count % 2 == 0
    if fused:
        whole_inputs, target_stats, acts_stack = encode(
            inputs_local,
            wanted,
            weight_enc,
            enc_bias[0].astype(F32)[:, None],
            active_mask[0],
            lat_count,
            layer_count,
        )
        whole_inputs = whole_inputs.reshape(feature_count, token_count)
        spread = jnp.sum(target_stats[:, 0, 0]) / total_cells + EPSILON
        stack_rows = acts_stack.reshape(layer_count * lat_rows, token_count)
        full_grad, err_stats, grad_rows = decode(
            dec_weight[0],
            acts_stack,
            wanted,
            dec_bias[0].astype(F32)[None, :],
            kept_tokens[:, None],
            jnp.broadcast_to(spread, (1, feature_rows)),
            lat_count,
        )
    else:
        whole_inputs, target_stats = gather_inputs(inputs_local, wanted, lat_count)
        whole_inputs = whole_inputs.reshape(feature_count, token_count)
        spread = jnp.sum(target_stats[:, 0, 0]) / total_cells + EPSILON
        preact = jnp.dot(weight_enc, whole_inputs, preferred_element_type=F32)
        preact = preact + enc_bias[0].astype(F32)[:, None]
        latents = (gating * preact).astype(BF16)
        gathered = lax.all_gather(latents[None], "layer", axis=0, tiled=True)
        acts_stack = jnp.where(
            (source_ids <= layer_here)[:, None, None], gathered, jnp.zeros((), BF16)
        )
        stack_rows = acts_stack.reshape(layer_count * lat_rows, token_count)
        parts = lax.dot_general(
            weight_rows, stack_rows, (((0,), (0,)), ((), ())), preferred_element_type=F32
        ).astype(BF16)
        full_grad, err_stats = reduce_and_gather(
            parts.reshape(lat_count, feature_rows, token_count),
            wanted,
            dec_bias[0].astype(F32)[:, None],
            kept_tokens[None, :],
            jnp.broadcast_to(spread, (1, token_count)),
            lat_count,
        )
    full_grad = full_grad.reshape(feature_count, token_count)
    layer_loss = jnp.sum(err_stats[:, 0, 0]) / (2.0 * spread * total_cells)
    total_loss = lax.psum(layer_loss, "layer")
    if not fused:
        grad_rows = jnp.dot(weight_rows, full_grad, preferred_element_type=F32).reshape(
            layer_count, lat_rows, token_count
        )
        grad_rows = (grad_rows * (source_ids <= layer_here).astype(F32)[:, None, None]).astype(BF16)
    dec_out = lax.dot_general(
        stack_rows, full_grad, (((1,), (1,)), ((), ())), preferred_element_type=F32
    )
    dec_out = dec_out.astype(BF16).reshape(1, layer_count, lat_rows, feature_count)
    latent_grad = lax.psum_scatter(grad_rows, "layer", scatter_dimension=0, tiled=True)[0]
    preact_grad = (gating * latent_grad.astype(F32)).astype(BF16)
    enc_out = lax.dot_general(
        preact_grad, whole_inputs, (((1,), (1,)), ((), ())), preferred_element_type=F32
    )
    return (enc_out.astype(BF16)[None], dec_out, total_loss)


def solution(mesh):
    in_specs = (
        P("layer", "lat", None),
        P("layer", "lat", None),
        P(),
        P("layer", "lat", None),
        P("layer", "lat", None),
        P("layer", "lat"),
        P("layer", None, "lat", None),
        P("layer", "lat"),
    )
    out_specs = (P("layer", "lat", None), P("layer", None, "lat", None), P())
    return jax.shard_map(
        on_device, mesh=mesh, in_specs=in_specs, out_specs=out_specs, check_vma=False
    )
```

```python
import functools

import jax
import jax.numpy as jnp
from jax import lax
from jax.experimental import pallas as pl
from jax.experimental.pallas import tpu as pltpu
from jax.sharding import PartitionSpec as P

EPSILON = 1e-05
F32 = jnp.float32
BF16 = jnp.bfloat16


class Place:
    def __init__(self, lat_count):
        self.me = lax.axis_index("lat")
        self.depth = lat_count // 2
        self.z = self.me // 2
        self.y = self.me % 2
        self.partner = self.me + 1 - 2 * self.y
        self.has_up = self.z < self.depth - 1
        self.has_down = self.z > 0


def send(src, dst, send_sem, recv_sem, lat):
    return pltpu.make_async_remote_copy(
        src_ref=src,
        dst_ref=dst,
        send_sem=send_sem,
        recv_sem=recv_sem,
        device_id={"lat": lat},
        device_id_type=pl.DeviceIdType.MESH,
    )


def greet(at, more=0):
    barrier = pltpu.get_barrier_semaphore()

    def hello(lat):
        pl.semaphore_signal(
            barrier, inc=1, device_id={"lat": lat}, device_id_type=pl.DeviceIdType.MESH
        )

    hello(at.partner)
    pl.when(at.has_up)(lambda: hello(at.me + 2))
    pl.when(at.has_down)(lambda: hello(at.me - 2))
    peers = 1 + more + at.has_up.astype(jnp.int32) + at.has_down.astype(jnp.int32)
    pl.semaphore_wait(barrier, peers)


class Gather:
    def __init__(self, at, own, whole, sems):
        self.at, self.own, self.whole, self.sems = at, own, whole, sems

    def hop(self, kind, d):
        at = self.at
        shard = at.me - 2 * d if kind in (0, 2) else at.me + 2 * d
        src = self.own if d == 0 else self.whole.at[shard]
        to = (at.me + 2, at.me - 2, at.partner, at.partner)[kind]
        later = d + 1 if kind < 2 else d
        return send(
            src, self.whole.at[shard], self.sems.at[0, kind, d], self.sems.at[1, kind, later], to
        )

    def landing(self, kind, d):
        at = self.at
        below = kind in (0, 2)
        shard = at.me - 2 * d if below else at.me + 2 * d
        if kind >= 2:
            shard = shard + 1 - 2 * at.y
        ref = self.whole.at[shard]
        return send(ref, ref, self.sems.at[0, kind, d], self.sems.at[1, kind, d], at.partner)

    def start(self):
        pl.when(self.at.has_up)(lambda: self.hop(0, 0).start())
        pl.when(self.at.has_down)(lambda: self.hop(1, 0).start())
        self.hop(2, 0).start()

    def step(self, d):
        at = self.at

        @pl.when(at.z >= d)
        def _():
            self.landing(0, d).wait_recv()
            pl.when(at.has_up)(lambda: self.hop(0, d).start())
            self.hop(2, d).start()

        @pl.when(at.z + d < at.depth)
        def _():
            self.landing(1, d).wait_recv()
            pl.when(at.has_down)(lambda: self.hop(1, d).start())
            self.hop(3, d).start()

    def finish(self, crossed=False):
        at = self.at
        for d in range(at.depth):

            @pl.when(at.z >= d)
            def _():
                if not crossed:
                    self.landing(2, d).wait_recv()
                self.hop(2, d).wait_send()
                if d < at.depth - 1:
                    pl.when(at.has_up)(lambda: self.hop(0, d).wait_send())

            @pl.when(at.z + d < at.depth)
            def _():
                if d > 0:
                    if not crossed:
                        self.landing(3, d).wait_recv()
                    self.hop(3, d).wait_send()
                if d < at.depth - 1:
                    pl.when(at.has_down)(lambda: self.hop(1, d).wait_send())


def gather_kernel(lat_count, own, wanted_ref, whole, stats, stat, big_sems, stat_sems, local_sem):
    at = Place(lat_count)
    greet(at)
    big = Gather(at, own, whole, big_sems)
    big.start()
    keep = pltpu.make_async_copy(own, whole.at[at.me], local_sem)
    keep.start()
    wanted = wanted_ref[...].astype(F32)
    centered = wanted - jnp.mean(wanted, axis=1, keepdims=True)
    total = jnp.sum(centered * centered, keepdims=True)
    stat[...] = jnp.broadcast_to(total, stat.shape)
    stats[at.me] = stat[...]
    small = Gather(at, stat, stats, stat_sems)
    small.start()
    for d in range(1, at.depth):
        big.step(d)
        small.step(d)
    keep.wait()
    big.finish()
    small.finish()


def reduce_kernel(
    lat_count,
    parts,
    wanted_ref,
    bias_ref,
    kept_ref,
    spread_ref,
    whole,
    stats,
    across_up,
    across_down,
    from_below,
    from_above,
    going_up,
    going_down,
    total,
    grad,
    stat,
    across_sems,
    line_sems,
    big_sems,
    stat_sems,
):
    at = Place(lat_count)
    depth = at.depth
    greet(at)

    def across(up, d):
        rung = at.z + d if up else at.z - d
        row = 0 if up else 1
        return send(
            parts.at[rung * 2 + 1 - at.y],
            (across_up if up else across_down).at[d],
            across_sems.at[0, row, d],
            across_sems.at[1, row, d],
            at.partner,
        )

    def along(up, d):
        row = 0 if up else 1
        return send(
            (going_up if up else going_down).at[d],
            (from_below if up else from_above).at[d - 1],
            line_sems.at[0, row, d],
            line_sems.at[1, row, d - 1],
            at.me + 2 if up else at.me - 2,
        )

    def arrived(up, d):
        row = 0 if up else 1
        ref = (from_below if up else from_above).at[d]
        send(ref, ref, line_sems.at[0, row, d], line_sems.at[1, row, d], at.partner).wait_recv()

    for d in range(depth - 1, -1, -1):
        pl.when(at.z + d < depth)(lambda: across(True, d).start())
        if d:
            pl.when(at.z >= d)(lambda: across(False, d).start())

    def forward(up, d):
        across(up, d).wait_recv()
        rung = at.z + d if up else at.z - d
        crossed = across_up if up else across_down
        came = from_below if up else from_above
        going = going_up if up else going_down
        behind = at.has_down if up else at.has_up
        mine = parts.at[rung * 2 + at.y]

        @pl.when(behind)
        def _():
            if d < depth - 1:
                arrived(up, d)
                going[d] = (
                    mine[...].astype(F32) + crossed[d].astype(F32) + came[d].astype(F32)
                ).astype(BF16)

        @pl.when(jnp.logical_not(behind))
        def _():
            going[d] = (mine[...].astype(F32) + crossed[d].astype(F32)).astype(BF16)

        along(up, d).start()

    for d in range(depth - 1, 0, -1):
        pl.when(at.z + d < depth)(lambda: forward(True, d))
        pl.when(at.z >= d)(lambda: forward(False, d))
    across(True, 0).wait_recv()
    total[...] = (
        parts[at.me].astype(F32)
        + across_up[0].astype(F32)
        + (bias_ref[...] - wanted_ref[...].astype(F32))
    )

    @pl.when(at.has_down)
    def _():
        arrived(True, 0)
        total[...] += from_below[0].astype(F32)

    @pl.when(at.has_up)
    def _():
        arrived(False, 0)
        total[...] += from_above[0].astype(F32)

    err = kept_ref[...] * total[...]
    grad[...] = (err / spread_ref[...]).astype(BF16)
    whole[at.me] = grad[...]
    big = Gather(at, grad, whole, big_sems)
    big.start()
    stat[...] = jnp.broadcast_to(jnp.sum(err * err, keepdims=True), stat.shape)
    stats[at.me] = stat[...]
    small = Gather(at, stat, stats, stat_sems)
    small.start()
    for d in range(1, depth):
        big.step(d)
        small.step(d)
    big.finish()
    small.finish()
    for d in range(depth - 1, -1, -1):

        @pl.when(at.z + d < depth)
        def _():
            across(True, d).wait_send()
            if d:
                along(True, d).wait_send()

        if d:

            @pl.when(at.z >= d)
            def _():
                across(False, d).wait_send()
                along(False, d).wait_send()


def flow(at, gathers, use):
    use(at.me)

    def cross(d):
        @pl.when(at.z >= d)
        def _():
            for one in gathers:
                one.landing(2, d).wait_recv()
            use(at.partner - 2 * d)

        if d:

            @pl.when(at.z + d < at.depth)
            def _():
                for one in gathers:
                    one.landing(3, d).wait_recv()
                use(at.partner + 2 * d)

    for d in range(1, at.depth):
        for one in gathers:
            one.step(d)
        pl.when(at.z >= d)(lambda: use(at.me - 2 * d))
        pl.when(at.z + d < at.depth)(lambda: use(at.me + 2 * d))
        cross(d - 1)
    cross(at.depth - 1)
    for one in gathers:
        one.finish(crossed=True)


def to_layer(src, dst, send_sem, recv_sem, layer):
    return pltpu.make_async_remote_copy(
        src_ref=src,
        dst_ref=dst,
        send_sem=send_sem,
        recv_sem=recv_sem,
        device_id={"layer": layer},
        device_id_type=pl.DeviceIdType.MESH,
    )


def encode_kernel(
    lat_count,
    layer_count,
    own,
    wanted_ref,
    weight,
    bias_ref,
    gate_ref,
    whole,
    stats,
    acts,
    stat,
    wanted_here,
    gate_here,
    blocks,
    acc,
    big_sems,
    stat_sems,
    local_sems,
    block_sems,
    layer_sems,
):
    at = Place(lat_count)
    rows = own.shape[0]
    pairs = layer_count // 2
    layer = lax.axis_index("layer")
    pair, core = layer // 2, layer % 2
    mate = layer + 1 - 2 * core

    def load(g):
        return pltpu.make_async_copy(
            weight.at[:, pl.ds(g * rows, rows)], blocks.at[g], block_sems.at[g]
        )

    fetch = pltpu.make_async_copy(wanted_ref, wanted_here, local_sems.at[1])
    fetch.start()
    fetch_gate = pltpu.make_async_copy(gate_ref, gate_here, local_sems.at[2])
    for g in range(lat_count):
        load(g).start()
    fetch_gate.start()
    barrier = pltpu.get_barrier_semaphore()
    for k in range(1, pairs):
        other = lax.rem(pair + k, pairs) * 2 + core
        pl.semaphore_signal(
            barrier, inc=1, device_id={"layer": other}, device_id_type=pl.DeviceIdType.MESH
        )
    pl.semaphore_signal(
        barrier, inc=1, device_id={"layer": mate}, device_id_type=pl.DeviceIdType.MESH
    )
    greet(at, pairs)
    big = Gather(at, own, whole, big_sems)
    big.start()
    keep = pltpu.make_async_copy(own, whole.at[at.me], local_sems.at[0])
    keep.start()
    fetch.wait()
    wanted = wanted_here[...].astype(F32)
    centered = wanted - jnp.mean(wanted, axis=1, keepdims=True)
    spread = jnp.sum(centered * centered, keepdims=True)
    stat[...] = jnp.broadcast_to(spread, stat.shape)
    stats[at.me] = stat[...]
    small = Gather(at, stat, stats, stat_sems)
    small.start()
    acc[...] = jnp.broadcast_to(bias_ref[...], acc.shape)
    for g in range(lat_count):
        load(g).wait()
    keep.wait()

    def use(g):
        acc[...] += jnp.dot(blocks[g], whole[g], preferred_element_type=F32)

    flow(at, (big, small), use)
    fetch_gate.wait()
    acts[layer] = (gate_here[...].astype(F32) * acc[...]).astype(BF16)

    def over(k):
        ref = acts.at[layer]
        return to_layer(
            ref, ref, layer_sems.at[0, 0, k], layer_sems.at[1, 0, k], layer + 2 * k
        )

    def pass_on(k):
        ref = acts.at[layer - 2 * k]
        return to_layer(ref, ref, layer_sems.at[0, 1, k], layer_sems.at[1, 1, k], mate)

    def landed(kind, k):
        ref = acts.at[layer - 2 * k if kind == 0 else mate - 2 * k]
        sem = layer_sems.at[1, kind, k]
        return to_layer(ref, ref, layer_sems.at[0, kind, k], sem, mate)

    for k in range(1, pairs):
        pl.when(pair + k < pairs)(lambda: over(k).start())
    pl.when(core == 0)(lambda: pass_on(0).start())
    for k in range(1, pairs):

        @pl.when(pair + k < pairs)
        def _():
            empty = jnp.zeros(acts.shape[1:], BF16)
            acts[layer + 2 * k] = empty
            acts[mate + 2 * k] = empty

    @pl.when(core == 0)
    def _():
        acts[mate] = jnp.zeros(acts.shape[1:], BF16)

    for k in range(1, pairs):

        @pl.when(pair >= k)
        def _():
            landed(0, k).wait_recv()
            pass_on(k).start()

    pl.when(core == 1)(lambda: landed(1, 0).wait_recv())
    for k in range(1, pairs):

        @pl.when(pair >= k)
        def _():
            landed(1, k).wait_recv()
            pass_on(k).wait_send()

        pl.when(pair + k < pairs)(lambda: over(k).wait_send())
    pl.when(core == 0)(lambda: pass_on(0).wait_send())


def decode_kernel(
    lat_count,
    weight,
    acts,
    wanted_ref,
    bias_ref,
    ids_ref,
    spread_stats,
    whole,
    loss,
    own_term,
    terms,
    wanted_here,
    stats,
    losses,
    giving,
    given,
    blocks,
    turned,
    leaving_up,
    leaving_down,
    across_up,
    across_down,
    from_below,
    from_above,
    going_up,
    going_down,
    total,
    grad,
    stat,
    acc,
    wanted_sem,
    mate_sems,
    loss_sems,
    block_sems,
    across_sems,
    line_sems,
    big_sems,
    stat_sems,
):
    at = Place(lat_count)
    depth = at.depth
    layer_count, lat_rows, tokens = acts.shape
    width = blocks.shape[3]
    layer = lax.axis_index("layer")
    pairs = layer_count // 2
    pair, core = layer // 2, layer % 2
    mate = layer + 1 - 2 * core
    cells = lat_count * width * tokens

    def load(g):
        columns = pl.ds(pl.multiple_of(g * width, width), width)
        return pltpu.make_async_copy(weight.at[:, :, columns], blocks.at[g], block_sems.at[g])

    for cross in (True, False):
        for d in range(depth - 1, -1, -1):
            mine = at.partner if cross else at.me
            pl.when(at.z + d < depth)(lambda: load(mine + 2 * d).start())
            if d:
                pl.when(at.z >= d)(lambda: load(mine - 2 * d).start())
    fetch = pltpu.make_async_copy(wanted_ref, wanted_here, wanted_sem)
    fetch.start()
    barrier = pltpu.get_barrier_semaphore()
    for k in range(1, layer_count):
        other = lax.rem(layer + k, layer_count)
        pl.semaphore_signal(
            barrier, inc=1, device_id={"layer": other}, device_id_type=pl.DeviceIdType.MESH
        )
    greet(at, layer_count - 1)
    for source in range(layer_count):
        turned[source] = jnp.transpose(acts[source])

    def part(g):
        load(g).wait()
        got = jnp.dot(turned[0], blocks[g, 0], preferred_element_type=F32)
        for source in range(1, layer_count):
            got += jnp.dot(turned[source], blocks[g, source], preferred_element_type=F32)
        return got

    def across(up, d):
        row = 0 if up else 1
        return send(
            (leaving_up if up else leaving_down).at[d],
            (across_up if up else across_down).at[d],
            across_sems.at[0, row, d],
            across_sems.at[1, row, d],
            at.partner,
        )

    def along(up, d):
        row = 0 if up else 1
        return send(
            (going_up if up else going_down).at[d],
            (from_below if up else from_above).at[d - 1],
            line_sems.at[0, row, d],
            line_sems.at[1, row, d - 1],
            at.me + 2 if up else at.me - 2,
        )

    def arrived(up, d):
        row = 0 if up else 1
        ref = (from_below if up else from_above).at[d]
        send(ref, ref, line_sems.at[0, row, d], line_sems.at[1, row, d], at.partner).wait_recv()

    def leave(up, d):
        made = part(at.partner + 2 * d if up else at.partner - 2 * d)
        (leaving_up if up else leaving_down)[d] = made.astype(BF16)
        across(up, d).start()

    for d in range(depth - 1, -1, -1):
        pl.when(at.z + d < depth)(lambda: leave(True, d))
        if d:
            pl.when(at.z >= d)(lambda: leave(False, d))

    def forward(up, d):
        total[...] = part(at.me + 2 * d if up else at.me - 2 * d)
        across(up, d).wait_recv()
        total[...] += (across_up if up else across_down)[d].astype(F32)
        if d < depth - 1:

            @pl.when(at.has_down if up else at.has_up)
            def _():
                arrived(up, d)
                total[...] += (from_below if up else from_above)[d].astype(F32)

        (going_up if up else going_down)[d] = total[...].astype(BF16)
        along(up, d).start()

    for d in range(depth - 1, 0, -1):
        pl.when(at.z + d < depth)(lambda: forward(True, d))
        pl.when(at.z >= d)(lambda: forward(False, d))
    fetch.wait()
    goal = jnp.transpose(wanted_here[...].astype(F32))
    total[...] = part(at.me) + bias_ref[...].astype(F32) - goal
    across(True, 0).wait_recv()
    total[...] += across_up[0].astype(F32)

    @pl.when(at.has_down)
    def _():
        arrived(True, 0)
        total[...] += from_below[0].astype(F32)

    @pl.when(at.has_up)
    def _():
        arrived(False, 0)
        total[...] += from_above[0].astype(F32)

    err = (ids_ref[...] != 128000).astype(F32) * jnp.transpose(total[...])
    spread = jnp.sum(spread_stats[...], axis=0) / cells + EPSILON
    grad[...] = (err / jnp.max(spread, keepdims=True)).astype(BF16)
    big = Gather(at, grad, whole, big_sems)
    big.start()
    whole[at.me] = grad[...]
    stat[...] = jnp.broadcast_to(jnp.sum(err * err, keepdims=True), stat.shape)
    stats[at.me] = stat[...]
    small = Gather(at, stat, stats, stat_sems)
    small.start()
    acc[...] = jnp.zeros_like(acc)

    def use(g):
        @pl.loop(0, layer_count)
        def _(source):
            acc[source] += jnp.dot(blocks[g, source], whole[g], preferred_element_type=F32)

    flow(at, (big, small), use)
    losses[layer] = jnp.sum(stats[...], axis=0) / (2.0 * spread * cells)

    def tell(k):
        ref = losses.at[layer]
        other = lax.rem(layer + k, layer_count)
        return to_layer(ref, ref, loss_sems.at[0, k], loss_sems.at[1, k], other)

    def told(k):
        other = lax.rem(layer - k + layer_count, layer_count)
        ref = losses.at[other]
        return to_layer(ref, ref, loss_sems.at[0, k], loss_sems.at[1, k], other)

    def give(k):
        return to_layer(
            giving.at[k], given.at[k], mate_sems.at[0, k], mate_sems.at[1, k], mate
        )

    def hand(k):
        giving[k] = acc[mate - 2 * k].astype(BF16)
        give(k).start()

    for k in range(pairs - 1, 0, -1):
        pl.when(pair >= k)(lambda: hand(k))
    pl.when(core == 1)(lambda: hand(0))
    for k in range(1, layer_count):
        tell(k).start()
    own_term[...] = acc[layer]
    for k in range(pairs - 1, 0, -1):

        @pl.when(pair >= k)
        def _():
            give(k).wait_recv()
            terms[k - 1] = (acc[layer - 2 * k] + given[k].astype(F32)).astype(BF16)
            give(k).wait_send()

        @pl.when(pair < k)
        def _():
            terms[k - 1] = jnp.zeros(terms.shape[1:], BF16)

    @pl.when(core == 0)
    def _():
        give(0).wait_recv()
        own_term[...] += given[0].astype(F32)

    pl.when(core == 1)(lambda: give(0).wait_send())
    for k in range(1, layer_count):
        told(k).wait_recv()
        tell(k).wait_send()
    loss[...] = jnp.sum(losses[...], axis=0)
    for d in range(depth - 1, -1, -1):

        @pl.when(at.z + d < depth)
        def _():
            across(True, d).wait_send()
            if d:
                along(True, d).wait_send()

        if d:

            @pl.when(at.z >= d)
            def _():
                across(False, d).wait_send()
                along(False, d).wait_send()


VMEM = pl.BlockSpec(memory_space=pltpu.VMEM)
HBM = pl.BlockSpec(memory_space=pltpu.HBM)


def encode(inputs_local, wanted, weight, bias, gate, lat_count, layer_count):
    rows, tokens = inputs_local.shape
    lat_rows = weight.shape[0]
    depth = lat_count // 2
    return pl.pallas_call(
        functools.partial(encode_kernel, lat_count, layer_count),
        out_shape=(
            jax.ShapeDtypeStruct((lat_count, rows, tokens), BF16),
            jax.ShapeDtypeStruct((lat_count, 8, 128), F32),
            jax.ShapeDtypeStruct((layer_count, lat_rows, tokens), BF16),
        ),
        in_specs=[HBM, HBM, HBM, VMEM, HBM],
        out_specs=(VMEM,) * 3,
        scratch_shapes=[
            pltpu.VMEM((8, 128), F32),
            pltpu.VMEM((rows, tokens), BF16),
            pltpu.VMEM((lat_rows, tokens), jnp.int32),
            pltpu.VMEM((lat_count, lat_rows, rows), BF16),
            pltpu.VMEM((lat_rows, tokens), F32),
            pltpu.SemaphoreType.DMA((2, 4, depth + 1)),
            pltpu.SemaphoreType.DMA((2, 4, depth + 1)),
            pltpu.SemaphoreType.DMA((3,)),
            pltpu.SemaphoreType.DMA((lat_count,)),
            pltpu.SemaphoreType.DMA((2, 2, layer_count // 2)),
        ],
        compiler_params=pltpu.CompilerParams(
            collective_id=2, has_side_effects=True, vmem_limit_bytes=58 << 20
        ),
    )(inputs_local, wanted, weight, bias, gate)


def decode(weight, acts, wanted, bias, ids, spread_stats, lat_count):
    layer_count, lat_rows, tokens = acts.shape
    rows = wanted.shape[0]
    depth = lat_count // 2
    pairs = layer_count // 2
    slots = pltpu.VMEM((depth, tokens, rows), BF16)
    return pl.pallas_call(
        functools.partial(decode_kernel, lat_count),
        out_shape=(
            jax.ShapeDtypeStruct((lat_count, rows, tokens), BF16),
            jax.ShapeDtypeStruct((8, 128), F32),
            jax.ShapeDtypeStruct((lat_rows, tokens), F32),
            jax.ShapeDtypeStruct((pairs - 1, lat_rows, tokens), BF16),
        ),
        in_specs=[HBM, VMEM, HBM] + [VMEM] * 3,
        out_specs=(VMEM,) * 4,
        scratch_shapes=[
            pltpu.VMEM((rows, tokens), BF16),
            pltpu.VMEM((lat_count, 8, 128), F32),
            pltpu.VMEM((layer_count, 8, 128), F32),
            pltpu.VMEM((pairs, lat_rows, tokens), BF16),
            pltpu.VMEM((pairs, lat_rows, tokens), BF16),
            pltpu.VMEM((lat_count, layer_count, lat_rows, rows), BF16),
            pltpu.VMEM((layer_count, tokens, lat_rows), BF16),
        ]
        + [slots] * 8
        + [
            pltpu.VMEM((tokens, rows), F32),
            pltpu.VMEM((rows, tokens), BF16),
            pltpu.VMEM((8, 128), F32),
            pltpu.VMEM((layer_count, lat_rows, tokens), F32),
            pltpu.SemaphoreType.DMA,
            pltpu.SemaphoreType.DMA((2, pairs)),
            pltpu.SemaphoreType.DMA((2, layer_count)),
            pltpu.SemaphoreType.DMA((lat_count,)),
            pltpu.SemaphoreType.DMA((2, 2, depth)),
            pltpu.SemaphoreType.DMA((2, 2, depth)),
            pltpu.SemaphoreType.DMA((2, 4, depth + 1)),
            pltpu.SemaphoreType.DMA((2, 4, depth + 1)),
        ],
        compiler_params=pltpu.CompilerParams(
            collective_id=3, has_side_effects=True, vmem_limit_bytes=58 << 20
        ),
    )(weight, acts, wanted, bias, ids, spread_stats)


def gather_inputs(inputs_local, wanted, lat_count):
    rows, tokens = inputs_local.shape
    depth = lat_count // 2
    return pl.pallas_call(
        functools.partial(gather_kernel, lat_count),
        out_shape=(
            jax.ShapeDtypeStruct((lat_count, rows, tokens), BF16),
            jax.ShapeDtypeStruct((lat_count, 8, 128), F32),
        ),
        in_specs=[VMEM] * 2,
        out_specs=(VMEM, VMEM),
        scratch_shapes=[
            pltpu.VMEM((8, 128), F32),
            pltpu.SemaphoreType.DMA((2, 4, depth + 1)),
            pltpu.SemaphoreType.DMA((2, 4, depth + 1)),
            pltpu.SemaphoreType.DMA,
        ],
        compiler_params=pltpu.CompilerParams(
            collective_id=0, has_side_effects=True, vmem_limit_bytes=32 << 20
        ),
    )(inputs_local, wanted)


def reduce_and_gather(parts, wanted, bias, kept, spread, lat_count):
    _, rows, tokens = parts.shape
    depth = lat_count // 2
    slots = pltpu.VMEM((depth, rows, tokens), BF16)
    return pl.pallas_call(
        functools.partial(reduce_kernel, lat_count),
        out_shape=(
            jax.ShapeDtypeStruct((lat_count, rows, tokens), BF16),
            jax.ShapeDtypeStruct((lat_count, 8, 128), F32),
        ),
        in_specs=[VMEM] * 5,
        out_specs=(VMEM, VMEM),
        scratch_shapes=[slots] * 6
        + [
            pltpu.VMEM((rows, tokens), F32),
            pltpu.VMEM((rows, tokens), BF16),
            pltpu.VMEM((8, 128), F32),
            pltpu.SemaphoreType.DMA((2, 2, depth)),
            pltpu.SemaphoreType.DMA((2, 2, depth)),
            pltpu.SemaphoreType.DMA((2, 4, depth + 1)),
            pltpu.SemaphoreType.DMA((2, 4, depth + 1)),
        ],
        compiler_params=pltpu.CompilerParams(
            collective_id=1, has_side_effects=True, vmem_limit_bytes=40 << 20
        ),
    )(parts, wanted, bias, kept, spread)


def on_device(
    resid_in, resid_out, token_ids, active_mask, enc_weight, enc_bias, dec_weight, dec_bias
):
    layer_count = lax.axis_size("layer")
    lat_count = lax.axis_size("lat")
    layer_here = lax.axis_index("layer")
    inputs_local = resid_in[0]
    wanted = resid_out[0]
    weight_enc = enc_weight[0]
    lat_rows = weight_enc.shape[0]
    feature_count = weight_enc.shape[1]
    feature_rows, token_count = inputs_local.shape
    total_cells = feature_count * token_count
    kept_tokens = (token_ids != 128000).astype(F32)
    source_ids = jnp.arange(layer_count)
    gating = active_mask[0].astype(F32)
    weight_rows = dec_weight[0].reshape(layer_count * lat_rows, feature_count)
    pairs = layer_count // 2
    fused = feature_rows % 128 == 0 and lat_rows % 128 == 0 and layer_count == 2 * pairs
    fused = fused and pairs > 1
    if fused:
        whole_inputs, target_stats, acts_stack = encode(
            inputs_local,
            wanted,
            weight_enc,
            enc_bias[0].astype(F32)[:, None],
            active_mask[0],
            lat_count,
            layer_count,
        )
        whole_inputs = whole_inputs.reshape(feature_count, token_count)
        stack_rows = acts_stack.reshape(layer_count * lat_rows, token_count)
        full_grad, loss_tile, latent_grad, terms = decode(
            dec_weight[0],
            acts_stack,
            wanted,
            dec_bias,
            token_ids[None, :],
            target_stats,
            lat_count,
        )
    else:
        whole_inputs, target_stats = gather_inputs(inputs_local, wanted, lat_count)
        whole_inputs = whole_inputs.reshape(feature_count, token_count)
        spread = jnp.sum(target_stats[:, 0, 0]) / total_cells + EPSILON
        preact = jnp.dot(weight_enc, whole_inputs, preferred_element_type=F32)
        preact = preact + enc_bias[0].astype(F32)[:, None]
        latents = (gating * preact).astype(BF16)
        gathered = lax.all_gather(latents[None], "layer", axis=0, tiled=True)
        acts_stack = jnp.where(
            (source_ids <= layer_here)[:, None, None], gathered, jnp.zeros((), BF16)
        )
        stack_rows = acts_stack.reshape(layer_count * lat_rows, token_count)
        parts = lax.dot_general(
            weight_rows, stack_rows, (((0,), (0,)), ((), ())), preferred_element_type=F32
        ).astype(BF16)
        full_grad, err_stats = reduce_and_gather(
            parts.reshape(lat_count, feature_rows, token_count),
            wanted,
            dec_bias[0].astype(F32)[:, None],
            kept_tokens[None, :],
            jnp.broadcast_to(spread, (1, token_count)),
            lat_count,
        )
    full_grad = full_grad.reshape(feature_count, token_count)
    if fused:
        total_loss = loss_tile[0, 0]
        moved = [
            lax.ppermute(
                terms[k - 1],
                "layer",
                [(d, d - 2 * k) for d in range(2 * k, layer_count)],
            )
            for k in range(1, pairs)
        ]
    else:
        layer_loss = jnp.sum(err_stats[:, 0, 0]) / (2.0 * spread * total_cells)
        total_loss = lax.psum(layer_loss, "layer")
        grad_rows = jnp.dot(weight_rows, full_grad, preferred_element_type=F32).reshape(
            layer_count, lat_rows, token_count
        )
        grad_rows = (grad_rows * (source_ids <= layer_here).astype(F32)[:, None, None]).astype(BF16)
    dec_out = lax.dot_general(
        stack_rows, full_grad, (((1,), (1,)), ((), ())), preferred_element_type=F32
    )
    dec_out = dec_out.astype(BF16).reshape(1, layer_count, lat_rows, feature_count)
    if fused:
        for came in moved:
            latent_grad = latent_grad + came.astype(F32)
    else:
        latent_grad = lax.psum_scatter(grad_rows, "layer", scatter_dimension=0, tiled=True)[0]
    preact_grad = (gating * latent_grad.astype(F32)).astype(BF16)
    enc_out = lax.dot_general(
        preact_grad, whole_inputs, (((1,), (1,)), ((), ())), preferred_element_type=F32
    )
    return (enc_out.astype(BF16)[None], dec_out, total_loss)


def solution(mesh):
    in_specs = (
        P("layer", "lat", None),
        P("layer", "lat", None),
        P(),
        P("layer", "lat", None),
        P("layer", "lat", None),
        P("layer", "lat"),
        P("layer", None, "lat", None),
        P("layer", "lat"),
    )
    out_specs = (P("layer", "lat", None), P("layer", None, "lat", None), P())
    return jax.shard_map(
        on_device, mesh=mesh, in_specs=in_specs, out_specs=out_specs, check_vma=False
    )
```
